32 devices in a mesh: grp: 8 (over z, core), tp: 4 (over y, x).
Axes of the slice: x: 2, y: 2, z: 4, core: 2. Of those that a mesh axis runs over, the one named last changes fastest.
Arguments:
- stream: bfloat16 [2048, 2048], P(('grp', 'tp')), may hold values from -6 to 6
- lengths: int32 [6], replicated, may hold values from 1 to 1024, 2048 in all
- att_routes: int32 [2048, 2], P(('grp', 'tp')), may hold values from 0 to 7, all different within a row
- att_gate: bfloat16 [2048, 2], P(('grp', 'tp')), may hold values from 0.19921875 to 1
- mlp_routes: int32 [2048, 2], P(('grp', 'tp')), may hold values from 0 to 7, all different within a row; in each aligned block of 256 rows (0 to 255, 256 to 511, ...) at most 80 rows name the same one
- mlp_gate: bfloat16 [2048, 2], P(('grp', 'tp')), may hold values from 0.19921875 to 1
- gain_attn: float32 [2048], replicated, may hold values from 0.25 to 1.75
- gain_mlp: float32 [2048], replicated, may hold values from 0.25 to 1.75
- w_query: bfloat16 [8, 2048, 2048], P(None, None, 'tp')
- w_key: bfloat16 [2048, 2048], P(None, 'tp')
- w_value: bfloat16 [2048, 2048], P(None, 'tp'), may hold values from -0.125 to 0.125
- w_output: bfloat16 [8, 2048, 2048], P(None, 'tp'), may hold values from -0.125 to 0.125
- w_gate: bfloat16 [2048, 45056], P(None, ('grp', 'tp')), may hold values from -0.125 to 0.125
- w_up: bfloat16 [2048, 45056], P(None, ('grp', 'tp')), may hold values from -0.125 to 0.125
- w_down: bfloat16 [45056, 2048], P(('grp', 'tp')), may hold values from -0.078125 to 0.078125
- cache_in: bfloat16 [2048, 4, 2, 16, 128], P('grp', None, None, 'tp'), may hold values from -6 to 6
- page_table: int32 [128], P('grp'), may hold values from 0 to 127, as said below
Outputs:
- hidden_out: bfloat16 [2048, 2048], P('grp', 'tp')
- cache_out: bfloat16 [128, 16, 4, 2, 16, 128], P('grp', None, None, None, 'tp')
The draws below stay inside these ranges and needn't reach their ends.
Inputs may be any that keep to these rules, and one draw needn't show every extreme that they name: Request r takes the lengths[r] tokens after those of requests 0 to r - 1; they sum to 2048 and the longest has exactly 1024. `att_routes`: the 2 experts of a token differ. `mlp_routes`: the 2 experts of a token differ; in each aligned block of 256 rows no expert is named by more than 80 rows, a bound that some block reaches. `page_table`: a permutation; of the 16 pages of each aligned block of 16 pages, exactly 2 go to each aligned block of 16 slots.
All inputs are finite; a program needn't handle non-finite values.
Results may differ from the reference program's by a relative error of at most 0.014.
Values may be sent and summed in bfloat16 or wider, within the bound.
A program may use at most 192 MiB of HBM per device.

```python
import math
import jax
import jax.numpy as jnp
import numpy as np
from jax import lax

D = 2048
HEADS = 16
HD = 128
E_ATT = 8
E_MLP = 8
FF = 5632
TOPK = 2
TOK_DEV = 256
REQS = 6
PAGE = 16
CLAYERS = 4
TOKENS = 2048
MOST_LEN = 1024
CAP = 80
PPD = 16
PAIR = 2
PAGES = 128
N_GRP = 8


def key_matrix(key):
    return jax.random.normal(jax.random.fold_in(key, 7), (D, HEADS * HD), jnp.float32) * D ** (-0.5)


def draw_w_key(key, part):
    return key_matrix(key).astype(jnp.bfloat16)


def draw_w_query(key, part):
    noise_part = jax.random.normal(jax.random.fold_in(key, 8), (E_ATT, D, HEADS * HD), jnp.float32) * D ** (-0.5)
    return noise_part.astype(jnp.bfloat16)


def draw_page_table(key, part):
    blocks = PAGES // PPD
    source_keys = jax.random.split(jax.random.fold_in(key, 21), blocks)
    page_ranks = jax.vmap(lambda sub_key: jax.random.permutation(sub_key, PPD))(source_keys)
    owner_block = page_ranks // PAIR
    within = page_ranks % PAIR
    owner_keys = jax.random.split(jax.random.fold_in(key, 22), blocks)
    owner_order = jax.vmap(lambda sub_key: jax.random.permutation(sub_key, PPD))(owner_keys)
    source = jnp.arange(blocks, dtype=jnp.int32)[:, None]
    local_slot = owner_order[owner_block, source * PAIR + within]
    return (owner_block * PPD + local_slot).reshape(-1).astype(jnp.int32)


def block_levels(stream_key, shape, cuts, least, top_value):
    loudness = 1.0
    for dim, blocks in cuts:
        heights = jax.random.uniform(jax.random.fold_in(jax.random.fold_in(stream_key, 6), dim), (blocks,), jnp.float32, least / len(cuts), top_value / len(cuts))
        loudness = loudness * jnp.repeat(jnp.exp(heights), shape[dim] // blocks).reshape((-1,) + (1,) * (len(shape) - 1 - dim))
    return loudness


def picks_of(rng, rows, count, top, lift):
    ranking = jax.random.permutation(jax.random.fold_in(rng, 1), count)
    favour = ranking
    for power in range(3):
        favour = favour * favour // count
    favour = favour * lift // count
    lots = jax.random.randint(jax.random.fold_in(rng, 2), (rows, count), 0, 4096) + favour
    holders = jax.random.permutation(jax.random.fold_in(rng, 3), rows)[jnp.arange(count) % rows]
    lots = jnp.where(jnp.arange(rows)[:, None] == holders[None, :], 1 << 14, lots)
    priority = lots * count + jnp.arange(count)
    return lax.top_k(priority.astype(jnp.int32), top)[1].astype(jnp.int32)


def length_profile(number_of, total, reach, slope):
    loads = [(1 << 20) // math.isqrt(standing ** slope) + 1 for standing in range(2, number_of + 1)]
    surplus, counts = total - reach - (number_of - 1), [1] * (number_of - 1)
    while surplus > 0:
        movable = [i for i in range(number_of - 1) if counts[i] < reach]
        pool, remaining = sum([loads[i] for i in movable]), surplus
        for i in movable:
            extra = min(reach - counts[i], max(1, remaining * loads[i] // pool), surplus)
            counts[i] = counts[i] + extra
            surplus = surplus - extra
    return np.array([reach] + counts)


def ragged_sizes(key, amount, total, reach, skew):
    if amount == 2:
        one = jax.random.randint(key, (), max(1, total - reach), min(reach, total - 1) + 1)
        return jnp.stack([one, total - one])
    sizes = jnp.asarray(length_profile(amount, total, reach, skew), jnp.int32)
    pairs = (amount - 1) // 2
    source_of, sink = sizes[1:1 + 2 * pairs:2], sizes[2:2 + 2 * pairs:2]
    margin = jnp.minimum(source_of - 1, reach - sink)
    moved = jax.random.randint(jax.random.fold_in(key, 1), (pairs,), 0, 1 << 20) % (margin + 1)
    sizes = sizes.at[1:1 + 2 * pairs:2].set(source_of - moved).at[2:2 + 2 * pairs:2].set(sink + moved)
    return sizes[jax.random.permutation(jax.random.fold_in(key, 2), amount)]


def deal_out(rng, own, number, rows, count, top, most, lean):
    order = jax.random.permutation(rng, count)
    packed, ordinary = shares(count, rows * top, most, lean, True), shares(count, rows * top, most, lean, False)
    places = jnp.arange(count)

    def named(sizes, rotation):
        used = int((sizes > 0).sum())
        fixed = max(1, used // 4)
        moved = fixed + (places - fixed + rotation * (used - fixed)) % max(1, count - fixed)
        return jnp.zeros((count,), jnp.int32).at[order[jnp.where(places < fixed, places, moved)]].set(jnp.asarray(sizes, jnp.int32))

    sizes = jnp.where(number % 4 == 0, named(packed, number // 4), named(ordinary, number - number // 4 - 1))
    mixed = jax.random.permutation(jax.random.fold_in(own, 3), count)
    source_of, taker = mixed[0:count // 2 * 2:2], mixed[1:count // 2 * 2:2]
    room = jnp.minimum(sizes[source_of] - 1, most - sizes[taker]) // 2
    room = jnp.where((source_of == order[0]) | (taker == order[0]) | (sizes[taker] == 0), 0, jnp.maximum(room, 0))
    moved = jax.random.randint(jax.random.fold_in(own, 4), (count // 2,), 0, 1 << 20) % (room + 1)
    sizes = sizes.at[source_of].add(-moved).at[taker].add(moved)
    labels = jnp.searchsorted(jnp.cumsum(sizes), jnp.arange(rows * top), side="right").astype(jnp.int32)
    grid = labels.reshape(top, rows).T
    grid = grid[jax.random.permutation(jax.random.fold_in(own, 1), rows)]
    rotation = jax.random.randint(jax.random.fold_in(own, 2), (rows, 1), 0, top)
    return jnp.take_along_axis(grid, (jnp.arange(top)[None, :] + rotation) % top, axis=1)


def shares(amount, total, bound, lean, full):
    portions = [(1 << 20) // math.isqrt(rank ** lean) + 1 for rank in range(1, amount + 1)]
    largest = bound if full else min(bound, max(-(-total // amount), total * portions[0] // sum(portions)))
    least = 1 if total - largest >= amount - 1 else 0
    given, rest = [largest] + [least] * (amount - 1), total - largest - least * (amount - 1)
    while rest > 0:
        candidates = [i for i in range(1, amount) if given[i] < largest] or [i for i in range(1, amount) if given[i] < bound]
        mass, left = sum([portions[i] for i in candidates]), rest
        for i in candidates:
            extra = min(bound - given[i], max(1, left * portions[i] // mass), rest)
            given[i] = given[i] + extra
            rest = rest - extra
    return np.array(given)


def noise(key, dims, deviation, reach, cuts=(), held_as=jnp.bfloat16):
    array = deviation * jax.random.normal(key, dims, jnp.float32)
    if cuts:
        array = array * block_levels(key, dims, cuts, -0.22, 0.18)
    return jnp.clip(array, -reach, reach).astype(held_as)


def setup_inputs(seed: int = 0) -> dict:
    key_list = jax.random.split(jax.random.key(seed), 18)
    stream = noise(key_list[0], (TOKENS, D), 1.0, 6.0, ((0, 32),))
    lengths = ragged_sizes(key_list[1], REQS, TOKENS, MOST_LEN, 2).astype(jnp.int32)
    att_routes = picks_of(key_list[2], TOKENS, E_ATT, TOPK, 2048)
    att_gate = jnp.clip(0.19921875 + 0.80078125 * jax.random.uniform(key_list[3], (TOKENS, TOPK), jnp.float32) ** block_levels(key_list[3], (TOKENS, TOPK), ((0, 32),), -0.2, 0.2), 0.19921875, 1.0).astype(jnp.bfloat16)
    mlp_routes_keys = jax.random.split(jax.random.fold_in(key_list[4], 1), TOKENS // TOK_DEV)
    mlp_routes_turns = jax.random.permutation(jax.random.fold_in(key_list[4], 3), TOKENS // TOK_DEV)
    mlp_routes = jax.vmap(lambda own, number: deal_out(jax.random.fold_in(key_list[4], 2), own, number, TOK_DEV, E_MLP, TOPK, CAP, 1))(mlp_routes_keys, mlp_routes_turns).reshape((TOKENS, TOPK))
    mlp_gate = jnp.clip(0.19921875 + 0.80078125 * jax.random.uniform(key_list[5], (TOKENS, TOPK), jnp.float32) ** block_levels(key_list[5], (TOKENS, TOPK), ((0, 32),), -0.2, 0.2), 0.19921875, 1.0).astype(jnp.bfloat16)
    gain_attn = jnp.clip(1.0 + 0.15 * jax.random.normal(key_list[6], (D,), jnp.float32), 0.25, 1.75)
    gain_mlp = jnp.clip(1.0 + 0.15 * jax.random.normal(key_list[7], (D,), jnp.float32), 0.25, 1.75)
    w_query = draw_w_query(jax.random.fold_in(key_list[17], 71), 0)
    w_key = draw_w_key(jax.random.fold_in(key_list[17], 71), 0)
    w_value = noise(key_list[10], (D, HEADS * HD), D ** -0.5, 0.125, ((1, 4),))
    w_output = noise(key_list[11], (E_ATT, HEADS * HD, D), (HEADS * HD) ** -0.5, 0.125, ((1, 4),))
    w_gate = noise(key_list[12], (D, E_MLP * FF), D ** -0.5, 0.125, ((1, 32),))
    w_up = noise(key_list[13], (D, E_MLP * FF), D ** -0.5, 0.125, ((1, 32),))
    w_down = noise(key_list[14], (E_MLP * FF, D), FF ** -0.5, 0.078125, ((0, 32),))
    cache_in = noise(key_list[15], (TOKENS, CLAYERS, 2, HEADS, HD), 1.0, 6.0, ((0, 8), (3, 4)))
    page_table = draw_page_table(jax.random.fold_in(key_list[17], 71), 0)
    return {"stream": stream, "lengths": lengths, "att_routes": att_routes, "att_gate": att_gate, "mlp_routes": mlp_routes, "mlp_gate": mlp_gate, "gain_attn": gain_attn, "gain_mlp": gain_mlp, "w_query": w_query, "w_key": w_key, "w_value": w_value, "w_output": w_output, "w_gate": w_gate, "w_up": w_up, "w_down": w_down, "cache_in": cache_in, "page_table": page_table}


epsilon = 1e-06
rope_base = 10000.0
masked_score = -1e+30

def rms_rows(row_values, gain_vector):
    widened = row_values.astype(jnp.float32)
    mean_square = lax.optimization_barrier(jnp.mean(widened * widened, axis=-1, keepdims=True))
    return (widened * lax.rsqrt(mean_square + epsilon) * gain_vector).astype(jnp.bfloat16)

def request_start(token_index, lengths):
    request_ends = jnp.cumsum(lengths, dtype=jnp.int32)
    passed = request_ends[None, :] <= token_index[:, None]
    starts = lax.optimization_barrier(jnp.max(jnp.where(passed, request_ends[None, :], 0), axis=1)).astype(jnp.int32)
    return (starts, lax.optimization_barrier(jnp.sum(passed.astype(jnp.int32), axis=1)).astype(jnp.int32))

def rope_turn(head_values, position):
    half_width = head_values.shape[-1] // 2
    frequency = rope_base ** (-(jnp.arange(half_width, dtype=jnp.float32) * 2.0 / head_values.shape[-1]))
    angles = position.astype(jnp.float32)[:, None] * frequency[None, :]
    view_shape = (angles.shape[0],) + (1,) * (head_values.ndim - 2) + (half_width,)
    cosine = jnp.cos(angles).reshape(view_shape)
    sine_part = jnp.sin(angles).reshape(view_shape)
    front_half = head_values[..., :half_width]
    back_half = head_values[..., half_width:]
    return jnp.concatenate([front_half * cosine - back_half * sine_part, back_half * cosine + front_half * sine_part], axis=-1)

def reference(stream, lengths, att_routes, att_gate, mlp_routes, mlp_gate, gain_attn, gain_mlp, w_query, w_key, w_value, w_output, w_gate, w_up, w_down, cache_in, page_table):
    token_index = jnp.arange(TOKENS, dtype=jnp.int32)
    starts, request = request_start(token_index, lengths)
    position = token_index - starts
    normed = rms_rows(stream, gain_attn)
    key_rows = rope_turn(jnp.dot(normed, w_key, preferred_element_type=jnp.float32).reshape(TOKENS, HEADS, HD), position).astype(jnp.bfloat16)
    value_rows = jnp.dot(normed, w_value, preferred_element_type=jnp.float32).reshape(TOKENS, HEADS, HD).astype(jnp.bfloat16)

    def add_query(running, expert):
        projected = jnp.dot(normed, w_query[expert], preferred_element_type=jnp.float32)
        hit_mask = (att_routes == expert).astype(jnp.float32)
        return (running + hit_mask[:, :, None] * projected[:, None, :], None)
    query_sum = lax.scan(add_query, jnp.zeros((TOKENS, TOPK, HEADS * HD), jnp.float32), jnp.arange(E_ATT, dtype=jnp.int32))[0]
    query_rows = rope_turn(query_sum.reshape(TOKENS, TOPK, HEADS, HD), position).astype(jnp.bfloat16)
    key_wide = lax.optimization_barrier(key_rows).astype(jnp.float32)
    value_wide = lax.optimization_barrier(value_rows).astype(jnp.float32)
    query_wide = lax.optimization_barrier(query_rows).astype(jnp.float32)
    query_block = math.gcd(TOKENS, 512)
    score_scale = HD ** (-0.5)

    def attend_block(first_row):
        query_part = lax.dynamic_slice_in_dim(query_wide, first_row, query_block, 0)
        row_index = first_row + jnp.arange(query_block, dtype=jnp.int32)
        row_request = lax.dynamic_slice_in_dim(request, first_row, query_block, 0)
        allowed = (request[None, :] == row_request[:, None]) & (token_index[None, :] <= row_index[:, None])
        scores = jnp.einsum('tkhd,shd->tkhs', query_part, key_wide) * score_scale
        live_pairs = allowed[:, None, None, :]
        scores = jnp.where(live_pairs, scores, masked_score)
        row_max = lax.optimization_barrier(jnp.max(scores, axis=-1, keepdims=True))
        weights = jnp.where(live_pairs, jnp.exp(scores - row_max), 0.0)
        rounded = lax.optimization_barrier(weights.astype(jnp.bfloat16)).astype(jnp.float32)
        return jnp.einsum('tkhs,shd->tkhd', rounded, value_wide) / lax.optimization_barrier(jnp.sum(weights, axis=-1))[..., None]
    attended = lax.map(attend_block, jnp.arange(0, TOKENS, query_block, dtype=jnp.int32)).reshape(TOKENS, TOPK, HEADS * HD)
    gate_wide = att_gate.astype(jnp.float32)

    def add_output(running, expert):
        mix_weight = jnp.where(att_routes == expert, gate_wide, 0.0)
        expert_mix = lax.optimization_barrier(jnp.sum(mix_weight[:, :, None] * attended, axis=1)).astype(jnp.bfloat16)
        return (running + jnp.dot(expert_mix, w_output[expert], preferred_element_type=jnp.float32), None)
    head_sum = lax.scan(add_output, jnp.zeros((TOKENS, D), jnp.float32), jnp.arange(E_ATT, dtype=jnp.int32))[0]
    middle = (stream.astype(jnp.float32) + head_sum).astype(jnp.bfloat16)
    normed_mid = rms_rows(middle, gain_mlp)
    limit = N_GRP * CAP
    mlp_wide = mlp_gate.astype(jnp.float32)

    def add_expert(running, expert):
        chosen = jnp.any(mlp_routes == expert, axis=1)
        weight = lax.optimization_barrier(jnp.sum(jnp.where(mlp_routes == expert, mlp_wide, 0.0), axis=1))
        picked_ids = jnp.nonzero(chosen, size=limit, fill_value=0)[0].astype(jnp.int32)
        valid_rows = jnp.arange(limit, dtype=jnp.int32) < jnp.sum(chosen.astype(jnp.int32))
        picked_rows = jnp.take(normed_mid, picked_ids, axis=0)
        gate_part = jnp.dot(picked_rows, lax.dynamic_slice_in_dim(w_gate, expert * FF, FF, 1), preferred_element_type=jnp.float32)
        up_part = jnp.dot(picked_rows, lax.dynamic_slice_in_dim(w_up, expert * FF, FF, 1), preferred_element_type=jnp.float32)
        hidden = (jax.nn.silu(gate_part) * up_part).astype(jnp.bfloat16)
        expert_out = jnp.dot(hidden, lax.dynamic_slice_in_dim(w_down, expert * FF, FF, 0), preferred_element_type=jnp.float32)
        scaled = jnp.where(valid_rows[:, None], jnp.take(weight, picked_ids)[:, None] * expert_out, 0.0)
        return (running.at[picked_ids].add(scaled), None)
    mlp_sum = lax.scan(add_expert, jnp.zeros((TOKENS, D), jnp.float32), jnp.arange(E_MLP, dtype=jnp.int32))[0]
    hidden_out = (middle.astype(jnp.float32) + mlp_sum).astype(jnp.bfloat16)
    page_blocks = cache_in.reshape(PAGES, PAGE, CLAYERS, 2, HEADS, HD)
    cache_out = jnp.zeros_like(page_blocks).at[page_table].set(page_blocks)
    return (hidden_out, cache_out)
```

```python
import functools

import jax
import jax.numpy as jnp
from jax import lax
from jax.experimental import pallas as pl
from jax.experimental.pallas import tpu as pltpu
from jax.sharding import PartitionSpec as P

HD = 128
E_ATT = 8
E_MLP = 8
TOPK = 2
META = 128
MESH = pl.DeviceIdType.MESH
VMEM_LIMIT = 56 * 1024 * 1024


epsilon = 1e-06
rope_base = 10000.0
masked_score = -1e30

ANY = pl.BlockSpec(memory_space=pl.ANY)
VM = pl.BlockSpec(memory_space=pltpu.VMEM)


def params(collective=None):
    if collective is None:
        return pltpu.CompilerParams(vmem_limit_bytes=VMEM_LIMIT)
    return pltpu.CompilerParams(
        vmem_limit_bytes=VMEM_LIMIT, collective_id=collective, has_side_effects=True
    )


def turn_heads(values, cosine, sine, heads):
    parts = []
    for head in range(heads):
        part = values[:, head * HD : (head + 1) * HD]
        parts.append(part * cosine + pltpu.roll(part, HD // 2, 1) * sine)
    return jnp.concatenate(parts, axis=1)


def key_value_kernel(
    tp_count, stream, meta, gain, cosine, sine, w_key, w_value,
    normed, kvm, resid,
    rows_all, meta_all, wk, wv, wsem, send, recv, msend, mrecv,
):
    tp = lax.axis_index("tp")
    rows = stream.shape[0]
    width = wk.shape[1]
    load_k = pltpu.make_async_copy(w_key, wk, wsem.at[0])
    load_v = pltpu.make_async_copy(w_value, wv, wsem.at[1])
    load_k.start()
    load_v.start()
    barrier = pltpu.get_barrier_semaphore()
    for j in range(1, tp_count):
        pl.semaphore_signal(
            barrier, inc=1, device_id={"tp": (tp + j) % tp_count}, device_id_type=MESH
        )
    mine = pl.ds(pl.multiple_of(tp * rows, rows), rows)
    pl.semaphore_wait(barrier, tp_count - 1)
    copies = []
    for j in range(1, tp_count):
        peer = {"tp": (tp + j) % tp_count}
        copies.append(
            pltpu.make_async_remote_copy(
                stream, rows_all.at[mine], send.at[j - 1], recv.at[j - 1], peer, MESH
            )
        )
        copies.append(
            pltpu.make_async_remote_copy(
                meta, meta_all.at[mine], msend.at[j - 1], mrecv.at[j - 1], peer, MESH
            )
        )
    for copy in copies:
        copy.start()
    rows_all[mine, :] = stream[...]
    meta_all[mine, :] = meta[...]
    for copy in copies:
        copy.wait()
    widened = rows_all[...].astype(jnp.float32)
    mean_square = jnp.mean(widened * widened, axis=-1, keepdims=True)
    hidden = (widened * lax.rsqrt(mean_square + epsilon) * gain[...]).astype(jnp.bfloat16)
    normed[...] = hidden
    resid[...] = rows_all[:, pl.ds(pl.multiple_of(tp * width, 128), width)]
    kvm[:, 2 * width :] = meta_all[...]
    load_k.wait()
    keys = jnp.dot(hidden, wk[...], preferred_element_type=jnp.float32)
    kvm[:, :width] = turn_heads(keys, cosine[...], sine[...], width // HD).astype(jnp.bfloat16)
    load_v.wait()
    values = jnp.dot(hidden, wv[...], preferred_element_type=jnp.float32)
    kvm[:, width : 2 * width] = values.astype(jnp.bfloat16)


def query_kernel(normed, meta, cosine, sine, w_query, query, total):
    expert = pl.program_id(0)
    width = w_query.shape[2]

    @pl.when(expert == 0)
    def _():
        total[...] = jnp.zeros_like(total)

    projected = jnp.dot(normed[...], w_query[0], preferred_element_type=jnp.float32)
    ids = meta[...].astype(jnp.float32)
    wanted = expert.astype(jnp.float32)
    for k in range(TOPK):
        total[k] = jnp.where(ids[:, k : k + 1] == wanted, projected, total[k])

    @pl.when(expert == E_ATT - 1)
    def _():
        for k in range(TOPK):
            query[k] = turn_heads(total[k], cosine[...], sine[...], width // HD).astype(
                jnp.bfloat16
            )


def attend_kernel(
    tp_count, grp_count, query, starts, meta, resid, kv_all, w_out,
    middle,
    kv, wo, att, mixed, outgoing, incoming, kvsem, wsem, send, recv,
):
    tp = lax.axis_index("tp")
    grp = lax.axis_index("grp")
    tok, width = resid.shape
    window = kv.shape[0]
    reach = grp_count // 2
    base = (grp // reach) * (grp - reach)
    load_kv = pltpu.make_async_copy(
        kv_all.at[pl.ds(pl.multiple_of(base * tok, tok), window), pl.ds(0, 2 * width)],
        kv, kvsem.at[0],
    )
    load_kv.start()
    load_w = [
        pltpu.make_async_copy(w_out.at[e], wo.at[pl.ds(e * width, width)], wsem.at[e])
        for e in range(E_ATT)
    ]
    for load in load_w:
        load.start()
    barrier = pltpu.get_barrier_semaphore()
    for j in range(1, tp_count):
        pl.semaphore_signal(
            barrier, inc=1, device_id={"tp": (tp + j) % tp_count}, device_id_type=MESH
        )
    column = lax.broadcasted_iota(jnp.int32, (tok, window), 1) + base * tok
    row = lax.broadcasted_iota(jnp.int32, (tok, window), 0) + grp * tok
    live = (column <= row) & (column >= starts[...])
    bias = jnp.where(live, 0.0, masked_score)
    load_kv.wait()
    scale = HD ** (-0.5)
    for head in range(width // HD):
        lanes = slice(head * HD, (head + 1) * HD)
        key_head = kv[:, lanes]
        value_head = kv[:, width + head * HD : width + (head + 1) * HD]
        for k in range(TOPK):
            scores = lax.dot_general(
                query[k, :, lanes], key_head, (((1,), (1,)), ((), ())),
                preferred_element_type=jnp.float32,
            ) + bias
            top = jnp.max(scores, axis=-1, keepdims=True)
            weights = jnp.exp((scores - top) * scale)
            total = jnp.sum(weights, axis=-1, keepdims=True)
            summed = jnp.dot(
                weights.astype(jnp.bfloat16), value_head, preferred_element_type=jnp.float32
            )
            att[k, :, lanes] = summed / total
    info = meta[...].astype(jnp.float32)
    for e in range(E_ATT):
        mix = None
        for k in range(TOPK):
            gate = jnp.where(info[:, k : k + 1] == float(e), info[:, TOPK + k : TOPK + k + 1], 0.0)
            term = gate * att[k]
            mix = term if mix is None else mix + term
        mixed[:, e * width : (e + 1) * width] = mix.astype(jnp.bfloat16)
    for load in load_w:
        load.wait()
    pl.semaphore_wait(barrier, tp_count - 1)
    copies = []
    for j in list(range(1, tp_count)) + [0]:
        peer = (tp + j) % tp_count
        part = jnp.dot(
            mixed[...], wo[:, pl.ds(pl.multiple_of(peer * width, 128), width)],
            preferred_element_type=jnp.float32,
        )
        if j:
            outgoing[j - 1] = part.astype(jnp.bfloat16)
            copy = pltpu.make_async_remote_copy(
                outgoing.at[j - 1], incoming.at[j - 1], send.at[j - 1], recv.at[j - 1],
                {"tp": peer}, MESH,
            )
            copy.start()
            copies.append(copy)
    result = resid[...].astype(jnp.float32) + part
    for j, copy in enumerate(copies):
        copy.wait()
        result = result + incoming[j].astype(jnp.float32)
    middle[...] = result.astype(jnp.bfloat16)


def expert_kernel(
    tp_count, grp_count, cap, step_blocks,
    mid_all, select, mid, mix, gain, w_gate, w_up, w_down, pages,
    out, arrived,
    wg, wu, wd, gathered, xn, rs_own, rs_out, rs_in, ret_out, ret_in,
    wsem, self_sem, psend, precv, asend, arecv, rsend, rrecv, tsend, trecv,
):
    tp = lax.axis_index("tp")
    grp = lax.axis_index("grp")
    width = mid.shape[1]
    loads = [
        pltpu.make_async_copy(src, dst, wsem.at[i])
        for i, (src, dst) in enumerate(((w_gate, wg), (w_up, wu), (w_down, wd)))
    ]
    for load in loads:
        load.start()
    barrier = pltpu.get_barrier_semaphore()
    for j in range(1, tp_count):
        pl.semaphore_signal(
            barrier, inc=1, device_id={"tp": (tp + j) % tp_count}, device_id_type=MESH
        )
    for j in range(1, grp_count):
        pl.semaphore_signal(
            barrier, inc=1, device_id={"grp": (grp + j) % grp_count}, device_id_type=MESH
        )
    self_copy = pltpu.make_async_copy(pages.at[grp], arrived.at[grp], self_sem.at[0])
    self_copy.start()

    step_rows = step_blocks * cap
    steps = grp_count // step_blocks

    def pick(step):
        for i in range(step * step_blocks, (step + 1) * step_blocks):
            block = (grp + 1 + i) % grp_count
            rows = jnp.dot(select[block], mid_all[block], preferred_element_type=jnp.float32)
            gathered[tp, i * cap : (i + 1) * cap, :] = rows.astype(jnp.bfloat16)

    ag = []

    def spread(step):
        rows = pl.ds(step * step_rows, step_rows)
        ag.append([])
        for j in range(1, tp_count):
            copy = pltpu.make_async_remote_copy(
                gathered.at[tp, rows], gathered.at[tp, rows],
                asend.at[step, j - 1], arecv.at[step, j - 1],
                {"tp": (tp + j) % tp_count}, MESH,
            )
            copy.start()
            ag[step].append(copy)

    pick(0)
    pl.semaphore_wait(barrier, tp_count - 1 + grp_count - 1)
    spread(0)
    page_copies = []
    for j in range(1, grp_count):
        peer = (grp + j) % grp_count
        copy = pltpu.make_async_remote_copy(
            pages.at[peer], arrived.at[grp], psend.at[j - 1], precv.at[j - 1],
            {"grp": peer}, MESH,
        )
        copy.start()
        page_copies.append(copy)
    for step in range(1, steps):
        pick(step)
        spread(step)
    for load in loads:
        load.wait()

    rs = []
    ret = []

    def give_back(step):
        rows = slice(step * step_rows, (step + 1) * step_rows)
        total = rs_own[rows, :]
        for j in range(tp_count - 1):
            rs[step][j].wait_recv()
            total = total + rs_in[j, rows, :].astype(jnp.float32)
        ret_out[rows, :] = total.astype(jnp.bfloat16)
        for i in range(step * step_blocks, (step + 1) * step_blocks):
            part = slice(i * cap, (i + 1) * cap)
            mine = pl.ds(pl.multiple_of(grp * cap, cap), cap)
            if i == grp_count - 1:
                ret_in[mine, :] = ret_out[part, :]
            else:
                copy = pltpu.make_async_remote_copy(
                    ret_out.at[pl.ds(i * cap, cap)], ret_in.at[mine],
                    tsend.at[i], trecv.at[i],
                    {"grp": (grp + 1 + i) % grp_count}, MESH,
                )
                copy.start()
                ret.append(copy)

    for step in range(steps):
        rows = slice(step * step_rows, (step + 1) * step_rows)
        for copy in ag[step]:
            copy.wait_recv()
        square = None
        for s in range(tp_count):
            part = gathered[s, rows, :].astype(jnp.float32)
            term = jnp.sum(part * part, axis=-1, keepdims=True)
            square = term if square is None else square + term
        factor = lax.rsqrt(square * (1.0 / (tp_count * width)) + epsilon)
        for s in range(tp_count):
            lanes = slice(s * width, (s + 1) * width)
            xn[:, lanes] = (
                gathered[s, rows, :].astype(jnp.float32) * factor * gain[:, lanes]
            ).astype(jnp.bfloat16)
        gate = jnp.dot(xn[...], wg[...], preferred_element_type=jnp.float32)
        up = jnp.dot(xn[...], wu[...], preferred_element_type=jnp.float32)
        hidden = (gate / (1.0 + jnp.exp(-gate)) * up).astype(jnp.bfloat16)
        rs.append([])
        for j in list(range(1, tp_count)) + [0]:
            peer = (tp + j) % tp_count
            part = jnp.dot(
                hidden, wd[:, pl.ds(pl.multiple_of(peer * width, 128), width)],
                preferred_element_type=jnp.float32,
            )
            if j:
                rs_out[j - 1, rows, :] = part.astype(jnp.bfloat16)
                span = pl.ds(step * step_rows, step_rows)
                copy = pltpu.make_async_remote_copy(
                    rs_out.at[j - 1, span], rs_in.at[j - 1, span],
                    rsend.at[step, j - 1], rrecv.at[step, j - 1],
                    {"tp": peer}, MESH,
                )
                copy.start()
                rs[step].append(copy)
            else:
                rs_own[rows, :] = part
        if step:
            give_back(step - 1)
    give_back(steps - 1)
    for copy in ret:
        copy.wait()
    for group in ag + rs:
        for copy in group:
            copy.wait_send()
    out[...] = (
        mid[...].astype(jnp.float32)
        + jnp.dot(mix[...], ret_in[...], preferred_element_type=jnp.float32)
    ).astype(jnp.bfloat16)
    self_copy.wait()
    for copy in page_copies:
        copy.wait()


def pick_pages_kernel(order, pages, picked, sem):
    count = pages.shape[0]
    copies = [
        pltpu.make_async_copy(pages.at[order[i]], picked.at[i], sem.at[i]) for i in range(count)
    ]
    for copy in copies:
        copy.start()
    for copy in copies:
        copy.wait()


def on_device(
    stream,
    lengths,
    att_routes,
    att_gate,
    mlp_routes,
    mlp_gate,
    gain_attn,
    gain_mlp,
    w_query,
    w_key,
    w_value,
    w_output,
    w_gate,
    w_up,
    w_down,
    cache_in,
    page_table,
):
    grp_count = lax.axis_size("grp")
    tp_count = lax.axis_size("tp")
    grp_index = lax.axis_index("grp")
    rows, model_width = stream.shape
    tok = rows * tp_count
    total_tok = tok * grp_count
    width = w_key.shape[1]
    pages_dev = page_table.shape[0]
    bf16 = jnp.bfloat16
    f32 = jnp.float32
    dma = pltpu.SemaphoreType.DMA
    sds = jax.ShapeDtypeStruct

    query_index = grp_index * tok + jnp.arange(tok, dtype=jnp.int32)
    ends = jnp.sum(
        jnp.where(
            jnp.arange(lengths.shape[0])[None, :] <= jnp.arange(lengths.shape[0])[:, None],
            lengths[None, :], 0,
        ),
        axis=1,
    )
    passed = ends[None, :] <= query_index[:, None]
    starts = jnp.max(jnp.where(passed, ends[None, :], 0), axis=1, keepdims=True)
    position = (query_index[:, None] - starts).astype(f32)
    frequency = rope_base ** (-(jnp.arange(HD // 2, dtype=f32) * 2.0 / HD))
    angles = position * frequency[None, :]
    cos_half, sin_half = jnp.cos(angles), jnp.sin(angles)
    cosine = jnp.concatenate([cos_half, cos_half], axis=1)
    sine = jnp.concatenate([-sin_half, sin_half], axis=1)

    meta = jnp.concatenate(
        [
            att_routes.astype(bf16),
            att_gate,
            mlp_routes.astype(bf16),
            mlp_gate,
            jnp.broadcast_to(page_table.astype(bf16)[None, :], (rows, pages_dev)),
        ],
        axis=1,
    )
    meta = jnp.pad(meta, ((0, 0), (0, META - meta.shape[1])))

    normed, kvm, resid = pl.pallas_call(
        functools.partial(key_value_kernel, tp_count),
        out_shape=(
            sds((tok, model_width), bf16),
            sds((tok, 2 * width + META), bf16),
            sds((tok, width), bf16),
        ),
        in_specs=[VM] * 5 + [ANY] * 2,
        out_specs=(VM,) * 3,
        scratch_shapes=[
            pltpu.VMEM((tok, model_width), bf16),
            pltpu.VMEM((tok, META), bf16),
            pltpu.VMEM(w_key.shape, bf16),
            pltpu.VMEM(w_value.shape, bf16),
            dma((2,)),
            dma((tp_count - 1,)),
            dma((tp_count - 1,)),
            dma((tp_count - 1,)),
            dma((tp_count - 1,)),
        ],
        compiler_params=params(1),
        name="gather_key_value",
    )(stream, meta, gain_attn[None, :], cosine, sine, w_key, w_value)

    kv_all = lax.all_gather(kvm, "grp", axis=0, tiled=True)

    meta_block = 2 * width // META
    query = pl.pallas_call(
        query_kernel,
        grid=(E_ATT,),
        out_shape=sds((TOPK, tok, width), bf16),
        in_specs=[
            pl.BlockSpec((tok, model_width), lambda e: (0, 0)),
            pl.BlockSpec((tok, META), lambda e: (0, meta_block)),
            pl.BlockSpec((tok, HD), lambda e: (0, 0)),
            pl.BlockSpec((tok, HD), lambda e: (0, 0)),
            pl.BlockSpec((1, model_width, width), lambda e: (e, 0, 0)),
        ],
        out_specs=pl.BlockSpec((TOPK, tok, width), lambda e: (0, 0, 0)),
        scratch_shapes=[pltpu.VMEM((TOPK, tok, width), f32)],
        compiler_params=params(),
        name="query",
    )(normed, kvm, cosine, sine, w_query)

    info = kvm[:, 2 * width :]
    window = (grp_count // 2 + 1) * tok
    middle = pl.pallas_call(
        functools.partial(attend_kernel, tp_count, grp_count),
        out_shape=sds((tok, width), bf16),
        in_specs=[VM] * 4 + [ANY] * 2,
        out_specs=VM,
        scratch_shapes=[
            pltpu.VMEM((window, 2 * width), bf16),
            pltpu.VMEM((E_ATT * width, model_width), bf16),
            pltpu.VMEM((TOPK, tok, width), f32),
            pltpu.VMEM((tok, E_ATT * width), bf16),
            pltpu.VMEM((tp_count - 1, tok, width), bf16),
            pltpu.VMEM((tp_count - 1, tok, width), bf16),
            dma((1,)),
            dma((E_ATT,)),
            dma((tp_count - 1,)),
            dma((tp_count - 1,)),
        ],
        compiler_params=params(2),
        name="attend",
    )(query, starts, info, resid, kv_all, w_output)

    mid_all = lax.all_gather(middle, "grp", axis=0, tiled=False)

    capacity = tok * TOPK * 5 // (E_MLP * 4)
    per_owner = grp_count // E_MLP
    my_expert = (grp_index // per_owner).astype(f32)
    meta_all = kv_all[:, 2 * width :].reshape(grp_count, tok, META)
    lower = jnp.arange(tok)[:, None] < jnp.arange(tok)[None, :]
    lower = lower.astype(bf16)
    hit = jnp.any(meta_all[:, :, 4:6].astype(f32) == my_expert, axis=2)
    rank = jnp.dot(hit.astype(bf16), lower, preferred_element_type=f32).astype(jnp.int32)
    slot_ids = jnp.arange(capacity, dtype=jnp.int32)
    select = (
        hit[:, None, :] & (rank[:, None, :] == slot_ids[None, :, None])
    ).astype(bf16)
    own_ids = info[:, 4:6].astype(jnp.int32)
    own_gate = info[:, 6:8].astype(f32)
    owner_expert = jnp.arange(grp_count, dtype=jnp.int32) // per_owner
    own_hot = own_ids[:, :, None] == owner_expert[None, None, :]
    own_weight = jnp.sum(jnp.where(own_hot, own_gate[:, :, None], 0.0), axis=1)
    own_hit = jnp.any(own_hot, axis=1)
    own_rank = jnp.dot(lower.T, own_hit.astype(bf16), preferred_element_type=f32).astype(jnp.int32)
    mix = jnp.where(
        own_rank[:, :, None] == slot_ids[None, None, :], own_weight[:, :, None], 0.0
    ).astype(bf16).reshape(tok, grp_count * capacity)

    page_len = tok // pages_dev
    pair_pages = pages_dev // grp_count
    page_blocks = cache_in.reshape((pages_dev, page_len) + cache_in.shape[1:])
    page_ids = jnp.arange(pages_dev, dtype=jnp.int32)
    sort_key = (page_table // pages_dev) * pages_dev + page_ids
    place = jnp.sum((sort_key[None, :] < sort_key[:, None]).astype(jnp.int32), axis=1)
    page_order = jnp.sum(
        jnp.where(place[None, :] == page_ids[:, None], page_ids[None, :], 0), axis=1
    )
    move_pages = pl.pallas_call(
        pick_pages_kernel,
        out_shape=sds(page_blocks.shape, bf16),
        in_specs=[pl.BlockSpec(memory_space=pltpu.SMEM), ANY],
        out_specs=ANY,
        scratch_shapes=[dma((pages_dev,))],
        compiler_params=pltpu.CompilerParams(),
        name="pick_pages",
    )
    page_sends = move_pages(page_order, page_blocks).reshape(
        (grp_count, pair_pages) + page_blocks.shape[1:]
    )

    hid = w_gate.shape[1]
    step_blocks = 2
    steps = grp_count // step_blocks
    slots = grp_count * capacity
    peers = tp_count - 1
    hidden_out, arrived = pl.pallas_call(
        functools.partial(expert_kernel, tp_count, grp_count, capacity, step_blocks),
        out_shape=(sds((tok, width), bf16), sds(page_sends.shape, bf16)),
        in_specs=[VM] * 5 + [ANY] * 4,
        out_specs=(VM, ANY),
        scratch_shapes=[
            pltpu.VMEM((model_width, hid), bf16),
            pltpu.VMEM((model_width, hid), bf16),
            pltpu.VMEM((hid, model_width), bf16),
            pltpu.VMEM((tp_count, slots, width), bf16),
            pltpu.VMEM((step_blocks * capacity, model_width), bf16),
            pltpu.VMEM((slots, width), f32),
            pltpu.VMEM((peers, slots, width), bf16),
            pltpu.VMEM((peers, slots, width), bf16),
            pltpu.VMEM((slots, width), bf16),
            pltpu.VMEM((slots, width), bf16),
            dma((3,)),
            dma((1,)),
            dma((grp_count - 1,)),
            dma((grp_count - 1,)),
            dma((steps, peers)),
            dma((steps, peers)),
            dma((steps, peers)),
            dma((steps, peers)),
            dma((grp_count - 1,)),
            dma((grp_count - 1,)),
        ],
        compiler_params=params(3),
        name="experts",
    )(mid_all, select, middle, mix, gain_mlp[None, :], w_gate, w_up, w_down, page_sends)

    tables = meta_all[:, 0, 8 : 8 + pages_dev].astype(jnp.int32).reshape(-1)
    here = tables // pages_dev == grp_index
    all_ids = jnp.arange(tables.shape[0], dtype=jnp.int32)
    arrival = jnp.sum(
        (here[None, :] & (all_ids[None, :] < all_ids[:, None])).astype(jnp.int32), axis=1
    )
    local = tables % pages_dev
    slot_source = jnp.sum(
        jnp.where(here[None, :] & (local[None, :] == page_ids[:, None]), arrival[None, :], 0),
        axis=1,
    )
    cache_out = move_pages(slot_source, arrived.reshape(page_blocks.shape))
    return (hidden_out, cache_out)


def solution(mesh):
    return jax.shard_map(
        on_device,
        mesh=mesh,
        in_specs=(
            P(("grp", "tp"), None),
            P(),
            P(("grp", "tp"), None),
            P(("grp", "tp"), None),
            P(("grp", "tp"), None),
            P(("grp", "tp"), None),
            P(),
            P(),
            P(None, None, "tp"),
            P(None, "tp"),
            P(None, "tp"),
            P(None, "tp", None),
            P(None, ("grp", "tp")),
            P(None, ("grp", "tp")),
            P(("grp", "tp"), None),
            P("grp", None, None, "tp", None),
            P("grp"),
        ),
        out_specs=(P("grp", "tp"), P("grp", None, None, None, "tp", None)),
        check_vma=False,
    )
```

```python
import functools

import jax
import jax.numpy as jnp
from jax import lax
from jax.experimental import pallas as pl
from jax.experimental.pallas import tpu as pltpu
from jax.sharding import PartitionSpec as P

HD = 128
E_ATT = 8
E_MLP = 8
TOPK = 2
META = 128
MESH = pl.DeviceIdType.MESH
VMEM_LIMIT = 56 * 1024 * 1024


epsilon = 1e-06
rope_base = 10000.0
masked_score = -1e30

ANY = pl.BlockSpec(memory_space=pl.ANY)
VM = pl.BlockSpec(memory_space=pltpu.VMEM)


def params(collective=None):
    if collective is None:
        return pltpu.CompilerParams(vmem_limit_bytes=VMEM_LIMIT)
    return pltpu.CompilerParams(
        vmem_limit_bytes=VMEM_LIMIT, collective_id=collective, has_side_effects=True
    )


def turn_heads(values, cosine, sine, heads):
    parts = []
    for head in range(heads):
        part = values[:, head * HD : (head + 1) * HD]
        parts.append(part * cosine + pltpu.roll(part, HD // 2, 1) * sine)
    return jnp.concatenate(parts, axis=1)


def key_value_kernel(
    tp_count, stream, meta, gain, cosine, sine, w_key, w_value,
    normed, kvm, info, resid,
    rows_all, wk, wv, wsem, send, recv, msend, mrecv,
):
    tp = lax.axis_index("tp")
    rows = stream.shape[0]
    width = wk.shape[1]
    load_k = pltpu.make_async_copy(w_key, wk, wsem.at[0])
    load_v = pltpu.make_async_copy(w_value, wv, wsem.at[1])
    load_k.start()
    load_v.start()
    barrier = pltpu.get_barrier_semaphore()
    for j in range(1, tp_count):
        pl.semaphore_signal(
            barrier, inc=1, device_id={"tp": (tp + j) % tp_count}, device_id_type=MESH
        )
    mine = pl.ds(pl.multiple_of(tp * rows, rows), rows)
    pl.semaphore_wait(barrier, tp_count - 1)
    copies = []
    for j in range(1, tp_count):
        peer = {"tp": (tp + j) % tp_count}
        copies.append(
            pltpu.make_async_remote_copy(
                stream, rows_all.at[mine], send.at[j - 1], recv.at[j - 1], peer, MESH
            )
        )
        copies.append(
            pltpu.make_async_remote_copy(
                meta, info.at[mine], msend.at[j - 1], mrecv.at[j - 1], peer, MESH
            )
        )
    for copy in copies:
        copy.start()
    rows_all[mine, :] = stream[...]
    info[mine, :] = meta[...]
    for copy in copies:
        copy.wait()
    widened = rows_all[...].astype(jnp.float32)
    mean_square = jnp.mean(widened * widened, axis=-1, keepdims=True)
    hidden = (widened * lax.rsqrt(mean_square + epsilon) * gain[...]).astype(jnp.bfloat16)
    normed[...] = hidden
    resid[...] = rows_all[:, pl.ds(pl.multiple_of(tp * width, 128), width)]
    load_k.wait()
    keys = jnp.dot(hidden, wk[...], preferred_element_type=jnp.float32)
    kvm[:, :width] = turn_heads(keys, cosine[...], sine[...], width // HD).astype(jnp.bfloat16)
    load_v.wait()
    values = jnp.dot(hidden, wv[...], preferred_element_type=jnp.float32)
    kvm[:, width : 2 * width] = values.astype(jnp.bfloat16)


def send_pages(grp_count, half, pages, arrived, self_sem, psend, precv):
    grp = lax.axis_index("grp")
    copies = [pltpu.make_async_copy(pages.at[grp, half], arrived.at[grp], self_sem.at[0])]
    for j in range(1, grp_count):
        peer = (grp + j) % grp_count
        copies.append(
            pltpu.make_async_remote_copy(
                pages.at[peer, half], arrived.at[grp], psend.at[j - 1], precv.at[j - 1],
                {"grp": peer}, MESH,
            )
        )
    for copy in copies:
        copy.start()
    return copies


def attend_kernel(
    tp_count, grp_count, first,
    normed, cosine, sine, starts, meta, resid, own_kv, table, w_query, w_out, pages,
    middle, arrived, tables,
    wq, wo, kv, total, query, att, mixed, outgoing, incoming,
    qsem, wsem, ring_send, ring_recv, side_send, side_recv, send, recv,
    self_sem, psend, precv, tsend, trecv,
):
    tp = lax.axis_index("tp")
    grp = lax.axis_index("grp")
    core = grp % 2
    tok, width = resid.shape
    reach = grp_count // 2
    window = (reach + 1) * tok
    load_q = [pltpu.make_async_copy(w_query.at[e], wq.at[e], qsem.at[e]) for e in range(E_ATT)]
    load_w = [
        pltpu.make_async_copy(w_out.at[e], wo.at[pl.ds(e * width, width)], wsem.at[e])
        for e in range(E_ATT)
    ]
    for load in load_q + load_w:
        load.start()
    barrier = pltpu.get_barrier_semaphore()
    for j in range(1, tp_count):
        pl.semaphore_signal(
            barrier, inc=1, device_id={"tp": (tp + j) % tp_count}, device_id_type=MESH
        )
    for j in range(1, grp_count):
        pl.semaphore_signal(
            barrier, inc=1, device_id={"grp": (grp + j) % grp_count}, device_id_type=MESH
        )
    kv[reach] = own_kv[...]
    pl.semaphore_wait(barrier, tp_count - 1 + grp_count - 1)

    hops = reach // 2
    onward = {"grp": (grp + 2) % grp_count}
    other = {"grp": grp + 1 - 2 * core}

    def ring(h):
        return pltpu.make_async_remote_copy(
            kv.at[reach - 2 * h], kv.at[reach - 2 * h - 2],
            ring_send.at[h], ring_recv.at[h], onward, MESH,
        )

    def side(n):
        return pltpu.make_async_remote_copy(
            kv.at[reach - 2 * (core + n)], kv.at[reach - 1 - 2 * n],
            side_send.at[n], side_recv.at[n], other, MESH,
        )

    rings = [ring(h) for h in range(hops)]
    sides = [side(n) for n in range(hops)]
    rings[0].start()

    table_copies = []
    for j in range(1, grp_count):
        table_copies.append(
            pltpu.make_async_remote_copy(
                table, tables.at[grp], tsend.at[j - 1], trecv.at[j - 1],
                {"grp": (grp + j) % grp_count}, MESH,
            )
        )
    for copy in table_copies:
        copy.start()
    tables[grp] = table[...]

    ids = meta[...].astype(jnp.float32)
    total[...] = jnp.zeros_like(total)
    for e in range(E_ATT):
        load_q[e].wait()
        projected = jnp.dot(normed[...], wq[e], preferred_element_type=jnp.float32)
        for k in range(TOPK):
            total[k] = jnp.where(
                ids[:, first + k : first + k + 1] == float(e), projected, total[k]
            )
    for k in range(TOPK):
        query[k] = turn_heads(total[k], cosine[...], sine[...], width // HD).astype(jnp.bfloat16)
    column = lax.broadcasted_iota(jnp.int32, (tok, window), 1) + (grp - reach) * tok
    row = lax.broadcasted_iota(jnp.int32, (tok, window), 0) + grp * tok
    live = (column <= row) & (column >= starts[...])
    bias = jnp.where(live, 0.0, masked_score)
    for h in range(hops):
        rings[h].wait_recv()
        if h + 1 < hops:
            rings[h + 1].start()
        sides[h].start()
    for h in range(hops):
        sides[h].wait_recv()
    page_copies = send_pages(grp_count, slice(0, 1), pages, arrived, self_sem, psend, precv)
    scale = HD ** (-0.5)
    for head in range(width // HD):
        lanes = slice(head * HD, (head + 1) * HD)
        key_head = kv[:, :, lanes].reshape(window, HD)
        value_head = kv[:, :, width + head * HD : width + (head + 1) * HD].reshape(window, HD)
        for k in range(TOPK):
            scores = lax.dot_general(
                query[k, :, lanes], key_head, (((1,), (1,)), ((), ())),
                preferred_element_type=jnp.float32,
            ) + bias
            top = jnp.max(scores, axis=-1, keepdims=True)
            weights = jnp.exp((scores - top) * scale)
            weight_sum = jnp.sum(weights, axis=-1, keepdims=True)
            summed = jnp.dot(
                weights.astype(jnp.bfloat16), value_head, preferred_element_type=jnp.float32
            )
            att[k, :, lanes] = summed / weight_sum
    for e in range(E_ATT):
        mix = None
        for k in range(TOPK):
            at = first + k
            gate = jnp.where(
                ids[:, at : at + 1] == float(e), ids[:, at + TOPK : at + TOPK + 1], 0.0
            )
            term = gate * att[k]
            mix = term if mix is None else mix + term
        mixed[:, e * width : (e + 1) * width] = mix.astype(jnp.bfloat16)
    for load in load_w:
        load.wait()
    copies = []
    for j in list(range(1, tp_count)) + [0]:
        peer = (tp + j) % tp_count
        part = jnp.dot(
            mixed[...], wo[:, pl.ds(pl.multiple_of(peer * width, 128), width)],
            preferred_element_type=jnp.float32,
        )
        if j:
            outgoing[j - 1] = part.astype(jnp.bfloat16)
            copy = pltpu.make_async_remote_copy(
                outgoing.at[j - 1], incoming.at[j - 1], send.at[j - 1], recv.at[j - 1],
                {"tp": peer}, MESH,
            )
            copy.start()
            copies.append(copy)
    result = resid[...].astype(jnp.float32) + part
    for j, copy in enumerate(copies):
        copy.wait()
        result = result + incoming[j].astype(jnp.float32)
    middle[...] = result.astype(jnp.bfloat16)
    for copy in rings + sides:
        copy.wait_send()
    for copy in table_copies + page_copies:
        copy.wait()


def expert_kernel(
    tp_count, grp_count, cap, step_blocks,
    select, mid, mix, gain, w_gate, w_up, w_down, pages,
    out, arrived,
    wg, wu, wd, picked, gathered, xn, rs_own, rs_out, rs_in, ret_out, ret_in,
    wsem, self_sem, psend, precv, dsend, drecv, asend, arecv, rsend, rrecv, tsend, trecv,
):
    tp = lax.axis_index("tp")
    grp = lax.axis_index("grp")
    width = mid.shape[1]
    loads = [
        pltpu.make_async_copy(src, dst, wsem.at[i])
        for i, (src, dst) in enumerate(((w_gate, wg), (w_up, wu), (w_down, wd)))
    ]
    for load in loads:
        load.start()
    barrier = pltpu.get_barrier_semaphore()
    for j in range(1, tp_count):
        pl.semaphore_signal(
            barrier, inc=1, device_id={"tp": (tp + j) % tp_count}, device_id_type=MESH
        )
    for j in range(1, grp_count):
        pl.semaphore_signal(
            barrier, inc=1, device_id={"grp": (grp + j) % grp_count}, device_id_type=MESH
        )
    per_owner = grp_count // E_MLP
    step_rows = step_blocks * cap
    steps = grp_count // step_blocks

    picked_rows = None
    for e in range(E_MLP):
        picked_rows = jnp.dot(
            select[e * cap : (e + 1) * cap, :], mid[...], preferred_element_type=jnp.float32
        )
        picked[e] = picked_rows.astype(jnp.bfloat16)
    gathered[tp, 0:cap, :] = picked[grp // per_owner]
    pl.semaphore_wait(barrier, tp_count - 1 + grp_count - 1)
    dispatch = []
    for i in range(1, grp_count):
        peer = (grp + grp_count - i) % grp_count
        copy = pltpu.make_async_remote_copy(
            picked.at[peer // per_owner], gathered.at[tp, pl.ds(i * cap, cap)],
            dsend.at[i - 1], drecv.at[i - 1], {"grp": peer}, MESH,
        )
        copy.start()
        dispatch.append(copy)

    ag = []

    def spread(step):
        rows = pl.ds(step * step_rows, step_rows)
        ag.append([])
        for j in range(1, tp_count):
            copy = pltpu.make_async_remote_copy(
                gathered.at[tp, rows], gathered.at[tp, rows],
                asend.at[step, j - 1], arecv.at[step, j - 1],
                {"tp": (tp + j) % tp_count}, MESH,
            )
            copy.start()
            ag[step].append(copy)

    for step in range(steps):
        for i in range(step * step_blocks, (step + 1) * step_blocks):
            if i:
                dispatch[i - 1].wait_recv()
        spread(step)
        if step == 0:
            page_copies = send_pages(
                grp_count, slice(1, None), pages, arrived, self_sem, psend, precv
            ) if pages.shape[1] > 1 else []
    for load in loads:
        load.wait()

    rs = []
    ret = []

    def give_back(step):
        rows = slice(step * step_rows, (step + 1) * step_rows)
        total = rs_own[rows, :]
        for j in range(tp_count - 1):
            rs[step][j].wait_recv()
            total = total + rs_in[j, rows, :].astype(jnp.float32)
        ret_out[rows, :] = total.astype(jnp.bfloat16)
        for i in range(step * step_blocks, (step + 1) * step_blocks):
            part = slice(i * cap, (i + 1) * cap)
            mine = pl.ds(pl.multiple_of(grp * cap, cap), cap)
            if i == 0:
                ret_in[mine, :] = ret_out[part, :]
            else:
                copy = pltpu.make_async_remote_copy(
                    ret_out.at[pl.ds(i * cap, cap)], ret_in.at[mine],
                    tsend.at[i - 1], trecv.at[i - 1],
                    {"grp": (grp + i) % grp_count}, MESH,
                )
                copy.start()
                ret.append(copy)

    for step in range(steps):
        rows = slice(step * step_rows, (step + 1) * step_rows)
        for copy in ag[step]:
            copy.wait_recv()
        square = None
        for s in range(tp_count):
            part = gathered[s, rows, :].astype(jnp.float32)
            term = jnp.sum(part * part, axis=-1, keepdims=True)
            square = term if square is None else square + term
        factor = lax.rsqrt(square * (1.0 / (tp_count * width)) + epsilon)
        for s in range(tp_count):
            lanes = slice(s * width, (s + 1) * width)
            xn[:, lanes] = (
                gathered[s, rows, :].astype(jnp.float32) * factor * gain[:, lanes]
            ).astype(jnp.bfloat16)
        gate = jnp.dot(xn[...], wg[...], preferred_element_type=jnp.float32)
        up = jnp.dot(xn[...], wu[...], preferred_element_type=jnp.float32)
        hidden = (gate / (1.0 + jnp.exp(-gate)) * up).astype(jnp.bfloat16)
        rs.append([])
        for j in list(range(1, tp_count)) + [0]:
            peer = (tp + j) % tp_count
            part = jnp.dot(
                hidden, wd[:, pl.ds(pl.multiple_of(peer * width, 128), width)],
                preferred_element_type=jnp.float32,
            )
            if j:
                rs_out[j - 1, rows, :] = part.astype(jnp.bfloat16)
                span = pl.ds(step * step_rows, step_rows)
                copy = pltpu.make_async_remote_copy(
                    rs_out.at[j - 1, span], rs_in.at[j - 1, span],
                    rsend.at[step, j - 1], rrecv.at[step, j - 1],
                    {"tp": peer}, MESH,
                )
                copy.start()
                rs[step].append(copy)
            else:
                rs_own[rows, :] = part
        if step:
            give_back(step - 1)
    give_back(steps - 1)
    for copy in ret:
        copy.wait()
    for copy in dispatch:
        copy.wait_send()
    for group in ag + rs:
        for copy in group:
            copy.wait_send()
    out[...] = (
        mid[...].astype(jnp.float32)
        + lax.dot_general(
            mix[...], ret_in[...], (((0,), (0,)), ((), ())), preferred_element_type=jnp.float32
        )
    ).astype(jnp.bfloat16)
    for copy in page_copies:
        copy.wait()


def pick_pages_kernel(order, pages, picked, held, isem, osem):
    count = pages.shape[0]
    reads = [
        pltpu.make_async_copy(pages.at[order[i]], held.at[i], isem.at[i]) for i in range(count)
    ]
    writes = [pltpu.make_async_copy(held.at[i], picked.at[i], osem.at[i]) for i in range(count)]
    for copy in reads:
        copy.start()
    for read, write in zip(reads, writes):
        read.wait()
        write.start()
    for copy in writes:
        copy.wait()


def place_pages_kernel(slot_of, *refs):
    parts, (placed, held, isem, osem) = refs[:-4], refs[-4:]
    reads = []
    for part in parts:
        for i in range(part.shape[0]):
            at = len(reads)
            reads.append(pltpu.make_async_copy(part.at[i], held.at[at], isem.at[at]))
    writes = [
        pltpu.make_async_copy(held.at[i], placed.at[slot_of[i]], osem.at[i])
        for i in range(len(reads))
    ]
    for copy in reads:
        copy.start()
    for read, write in zip(reads, writes):
        read.wait()
        write.start()
    for copy in writes:
        copy.wait()


def on_device(
    stream,
    lengths,
    att_routes,
    att_gate,
    mlp_routes,
    mlp_gate,
    gain_attn,
    gain_mlp,
    w_query,
    w_key,
    w_value,
    w_output,
    w_gate,
    w_up,
    w_down,
    cache_in,
    page_table,
):
    grp_count = lax.axis_size("grp")
    tp_count = lax.axis_size("tp")
    grp_index = lax.axis_index("grp")
    rows, model_width = stream.shape
    tok = rows * tp_count
    total_tok = tok * grp_count
    width = w_key.shape[1]
    pages_dev = page_table.shape[0]
    bf16 = jnp.bfloat16
    f32 = jnp.float32
    dma = pltpu.SemaphoreType.DMA
    sds = jax.ShapeDtypeStruct

    query_index = grp_index * tok + jnp.arange(tok, dtype=jnp.int32)
    ends = jnp.sum(
        jnp.where(
            jnp.arange(lengths.shape[0])[None, :] <= jnp.arange(lengths.shape[0])[:, None],
            lengths[None, :], 0,
        ),
        axis=1,
    )
    passed = ends[None, :] <= query_index[:, None]
    starts = jnp.max(jnp.where(passed, ends[None, :], 0), axis=1, keepdims=True)
    position = (query_index[:, None] - starts).astype(f32)
    frequency = rope_base ** (-(jnp.arange(HD // 2, dtype=f32) * 2.0 / HD))
    angles = position * frequency[None, :]
    cos_half, sin_half = jnp.cos(angles), jnp.sin(angles)
    cosine = jnp.concatenate([cos_half, cos_half], axis=1)
    sine = jnp.concatenate([-sin_half, sin_half], axis=1)

    meta = jnp.concatenate(
        [
            att_routes.astype(bf16),
            att_gate,
            mlp_routes.astype(bf16),
            mlp_gate,
        ],
        axis=1,
    )
    meta = jnp.pad(meta, ((0, 0), (0, META - meta.shape[1])))

    normed, kvm, info, resid = pl.pallas_call(
        functools.partial(key_value_kernel, tp_count),
        out_shape=(
            sds((tok, model_width), bf16),
            sds((tok, 2 * width), bf16),
            sds((tok, META), bf16),
            sds((tok, width), bf16),
        ),
        in_specs=[VM] * 5 + [ANY] * 2,
        out_specs=(VM,) * 4,
        scratch_shapes=[
            pltpu.VMEM((tok, model_width), bf16),
            pltpu.VMEM(w_key.shape, bf16),
            pltpu.VMEM(w_value.shape, bf16),
            dma((2,)),
            dma((tp_count - 1,)),
            dma((tp_count - 1,)),
            dma((tp_count - 1,)),
            dma((tp_count - 1,)),
        ],
        compiler_params=params(1),
        name="gather_key_value",
    )(stream, meta, gain_attn[None, :], cosine, sine, w_key, w_value)

    page_len = tok // pages_dev
    pair_pages = pages_dev // grp_count
    page_blocks = cache_in.reshape((pages_dev, page_len) + cache_in.shape[1:])
    page_ids = jnp.arange(pages_dev, dtype=jnp.int32)
    sort_key = (page_table // pages_dev) * pages_dev + page_ids
    place = jnp.sum((sort_key[None, :] < sort_key[:, None]).astype(jnp.int32), axis=1)
    page_order = jnp.sum(
        jnp.where(place[None, :] == page_ids[:, None], page_ids[None, :], 0), axis=1
    )
    page_sends = pl.pallas_call(
        pick_pages_kernel,
        out_shape=sds(page_blocks.shape, bf16),
        in_specs=[pl.BlockSpec(memory_space=pltpu.SMEM), ANY],
        out_specs=ANY,
        scratch_shapes=[
            pltpu.VMEM(page_blocks.shape, bf16),
            dma((pages_dev,)),
            dma((pages_dev,)),
        ],
        compiler_params=params(),
        name="pick_pages",
    )(page_order, page_blocks).reshape(
        (grp_count, pair_pages) + page_blocks.shape[1:]
    )

    window = (grp_count // 2 + 1) * tok
    early_shape = (grp_count, 1) + page_blocks.shape[1:]
    reach = grp_count // 2
    peers = tp_count - 1
    table = jnp.broadcast_to(jnp.pad(page_table, (0, META - pages_dev))[None, :], (8, META))
    middle, early_pages, tables = pl.pallas_call(
        functools.partial(attend_kernel, tp_count, grp_count, 0),
        out_shape=(
            sds((tok, width), bf16),
            sds(early_shape, bf16),
            sds((grp_count, 8, META), jnp.int32),
        ),
        in_specs=[VM] * 8 + [ANY] * 3,
        out_specs=(VM, ANY, VM),
        scratch_shapes=[
            pltpu.VMEM(w_query.shape, bf16),
            pltpu.VMEM((E_ATT * width, model_width), bf16),
            pltpu.VMEM((reach + 1, tok, 2 * width), bf16),
            pltpu.VMEM((TOPK, tok, width), f32),
            pltpu.VMEM((TOPK, tok, width), bf16),
            pltpu.VMEM((TOPK, tok, width), f32),
            pltpu.VMEM((tok, E_ATT * width), bf16),
            pltpu.VMEM((peers, tok, width), bf16),
            pltpu.VMEM((peers, tok, width), bf16),
            dma((E_ATT,)),
            dma((E_ATT,)),
            dma((reach // 2,)),
            dma((reach // 2,)),
            dma((reach // 2,)),
            dma((reach // 2,)),
            dma((peers,)),
            dma((peers,)),
            dma((1,)),
            dma((grp_count - 1,)),
            dma((grp_count - 1,)),
            dma((grp_count - 1,)),
            dma((grp_count - 1,)),
        ],
        compiler_params=params(2),
        name="attend",
    )(normed, cosine, sine, starts, info, resid, kvm, table, w_query, w_output, page_sends)

    capacity = tok * TOPK * 5 // (E_MLP * 4)
    per_owner = grp_count // E_MLP
    lower = (jnp.arange(tok)[:, None] < jnp.arange(tok)[None, :]).astype(bf16)
    slot_ids = jnp.arange(capacity, dtype=jnp.int32)
    at = 2 * TOPK
    own_ids = info[:, at : at + TOPK].astype(jnp.int32).T
    own_gate = info[:, at + TOPK : at + 2 * TOPK].astype(f32).T
    expert_ids = jnp.arange(E_MLP, dtype=jnp.int32)
    own_hot = own_ids[None, :, :] == expert_ids[:, None, None]
    own_weight = jnp.sum(jnp.where(own_hot, own_gate[None, :, :], 0.0), axis=1)
    own_hit = jnp.any(own_hot, axis=1)
    own_rank = jnp.dot(own_hit.astype(bf16), lower, preferred_element_type=f32).astype(jnp.int32)
    placed = own_hit[:, None, :] & (own_rank[:, None, :] == slot_ids[None, :, None])
    select = placed.astype(bf16).reshape(E_MLP * capacity, tok)
    mix = jnp.where(placed, own_weight[:, None, :], 0.0).astype(bf16)
    mix = jnp.repeat(mix, per_owner, axis=0).reshape(grp_count * capacity, tok)

    hid = w_gate.shape[1]
    late_shape = (grp_count, max(pair_pages - 1, 1)) + page_blocks.shape[1:]
    step_blocks = 2
    steps = grp_count // step_blocks
    slots = grp_count * capacity
    peers = tp_count - 1
    hidden_out, late_pages = pl.pallas_call(
        functools.partial(expert_kernel, tp_count, grp_count, capacity, step_blocks),
        out_shape=(sds((tok, width), bf16), sds(late_shape, bf16)),
        in_specs=[VM] * 4 + [ANY] * 4,
        out_specs=(VM, ANY),
        scratch_shapes=[
            pltpu.VMEM((model_width, hid), bf16),
            pltpu.VMEM((model_width, hid), bf16),
            pltpu.VMEM((hid, model_width), bf16),
            pltpu.VMEM((E_MLP, capacity, width), bf16),
            pltpu.VMEM((tp_count, slots, width), bf16),
            pltpu.VMEM((step_blocks * capacity, model_width), bf16),
            pltpu.VMEM((slots, width), f32),
            pltpu.VMEM((peers, slots, width), bf16),
            pltpu.VMEM((peers, slots, width), bf16),
            pltpu.VMEM((slots, width), bf16),
            pltpu.VMEM((slots, width), bf16),
            dma((3,)),
            dma((1,)),
            dma((grp_count - 1,)),
            dma((grp_count - 1,)),
            dma((grp_count - 1,)),
            dma((grp_count - 1,)),
            dma((steps, peers)),
            dma((steps, peers)),
            dma((steps, peers)),
            dma((steps, peers)),
            dma((grp_count - 1,)),
            dma((grp_count - 1,)),
        ],
        compiler_params=params(3),
        name="experts",
    )(select, middle, mix, gain_mlp[None, :], w_gate, w_up, w_down, page_sends)

    tables = tables[:, 0, :pages_dev].reshape(-1)
    here = tables // pages_dev == grp_index
    all_ids = jnp.arange(tables.shape[0], dtype=jnp.int32)
    arrival = jnp.sum(
        (here[None, :] & (all_ids[None, :] < all_ids[:, None])).astype(jnp.int32), axis=1
    )
    source = arrival // pair_pages
    within = arrival % pair_pages
    arrival = jnp.where(
        within == 0, source, grp_count + source * (pair_pages - 1) + within - 1
    )
    local = tables % pages_dev
    slot_of = jnp.sum(
        jnp.where(here[None, :] & (arrival[None, :] == page_ids[:, None]), local[None, :], 0),
        axis=1,
    )
    parts = [early_pages] if pair_pages == 1 else [early_pages, late_pages]
    parts = [part.reshape((-1,) + page_blocks.shape[1:]) for part in parts]
    cache_out = pl.pallas_call(
        place_pages_kernel,
        out_shape=sds(page_blocks.shape, bf16),
        in_specs=[pl.BlockSpec(memory_space=pltpu.SMEM)] + [ANY] * len(parts),
        out_specs=ANY,
        scratch_shapes=[
            pltpu.VMEM(page_blocks.shape, bf16),
            dma((pages_dev,)),
            dma((pages_dev,)),
        ],
        compiler_params=params(),
        name="place_pages",
    )(slot_of, *parts)
    return (hidden_out, cache_out)


def solution(mesh):
    return jax.shard_map(
        on_device,
        mesh=mesh,
        in_specs=(
            P(("grp", "tp"), None),
            P(),
            P(("grp", "tp"), None),
            P(("grp", "tp"), None),
            P(("grp", "tp"), None),
            P(("grp", "tp"), None),
            P(),
            P(),
            P(None, None, "tp"),
            P(None, "tp"),
            P(None, "tp"),
            P(None, "tp", None),
            P(None, ("grp", "tp")),
            P(None, ("grp", "tp")),
            P(("grp", "tp"), None),
            P("grp", None, None, "tp", None),
            P("grp"),
        ),
        out_specs=(P("grp", "tp"), P("grp", None, None, None, "tp", None)),
        check_vma=False,
    )
```

```python
import functools

import jax
import jax.numpy as jnp
from jax import lax
from jax.experimental import pallas as pl
from jax.experimental.pallas import tpu as pltpu
from jax.sharding import PartitionSpec as P

HD = 128
E_ATT = 8
E_MLP = 8
TOPK = 2
META = 128
MESH = pl.DeviceIdType.MESH
VMEM_LIMIT = 56 * 1024 * 1024


epsilon = 1e-06
rope_base = 10000.0
masked_score = -1e30

ANY = pl.BlockSpec(memory_space=pl.ANY)
VM = pl.BlockSpec(memory_space=pltpu.VMEM)


def params(collective=None):
    if collective is None:
        return pltpu.CompilerParams(vmem_limit_bytes=VMEM_LIMIT)
    return pltpu.CompilerParams(
        vmem_limit_bytes=VMEM_LIMIT, collective_id=collective, has_side_effects=True
    )


def turn_heads(values, cosine, sine, heads):
    parts = []
    for head in range(heads):
        part = values[:, head * HD : (head + 1) * HD]
        parts.append(part * cosine + pltpu.roll(part, HD // 2, 1) * sine)
    return jnp.concatenate(parts, axis=1)


def key_value_kernel(
    tp_count, stream, att_routes, att_gate, mlp_routes, mlp_gate, gain, cosine, sine, w_key, w_value,
    normed, kvm, info, resid,
    rows_all, meta, wk, wv, wsem, send, recv, msend, mrecv,
):
    tp = lax.axis_index("tp")
    rows = stream.shape[0]
    width = wk.shape[1]
    load_k = pltpu.make_async_copy(w_key, wk, wsem.at[0])
    load_v = pltpu.make_async_copy(w_value, wv, wsem.at[1])
    load_k.start()
    load_v.start()
    barrier = pltpu.get_barrier_semaphore()
    for j in range(1, tp_count):
        pl.semaphore_signal(
            barrier, inc=1, device_id={"tp": (tp + j) % tp_count}, device_id_type=MESH
        )
    mine = pl.ds(pl.multiple_of(tp * rows, rows), rows)
    fields = [
        ref[...].astype(jnp.float32) for ref in (att_routes, att_gate, mlp_routes, mlp_gate)
    ]
    rest = jnp.zeros((rows, META - 4 * TOPK), jnp.float32)
    meta[...] = jnp.concatenate(fields + [rest], axis=1).astype(jnp.bfloat16)
    pl.semaphore_wait(barrier, tp_count - 1)
    copies = []
    for j in range(1, tp_count):
        peer = {"tp": (tp + j) % tp_count}
        copies.append(
            pltpu.make_async_remote_copy(
                stream, rows_all.at[mine], send.at[j - 1], recv.at[j - 1], peer, MESH
            )
        )
        copies.append(
            pltpu.make_async_remote_copy(
                meta, info.at[mine], msend.at[j - 1], mrecv.at[j - 1], peer, MESH
            )
        )
    for copy in copies:
        copy.start()
    rows_all[mine, :] = stream[...]
    info[mine, :] = meta[...]
    for copy in copies:
        copy.wait()
    widened = rows_all[...].astype(jnp.float32)
    mean_square = jnp.mean(widened * widened, axis=-1, keepdims=True)
    hidden = (widened * lax.rsqrt(mean_square + epsilon) * gain[...]).astype(jnp.bfloat16)
    normed[...] = hidden
    resid[...] = rows_all[:, pl.ds(pl.multiple_of(tp * width, 128), width)]
    load_k.wait()
    keys = jnp.dot(hidden, wk[...], preferred_element_type=jnp.float32)
    kvm[:, :width] = turn_heads(keys, cosine[...], sine[...], width // HD).astype(jnp.bfloat16)
    load_v.wait()
    values = jnp.dot(hidden, wv[...], preferred_element_type=jnp.float32)
    kvm[:, width : 2 * width] = values.astype(jnp.bfloat16)


def send_pages(grp_count, half, pages, arrived, self_sem, psend, precv):
    grp = lax.axis_index("grp")
    copies = [pltpu.make_async_copy(pages.at[grp, half], arrived.at[grp], self_sem.at[0])]
    for j in range(1, grp_count):
        peer = (grp + j) % grp_count
        copies.append(
            pltpu.make_async_remote_copy(
                pages.at[peer, half], arrived.at[grp], psend.at[j - 1], precv.at[j - 1],
                {"grp": peer}, MESH,
            )
        )
    for copy in copies:
        copy.start()
    return copies


def attend_kernel(
    tp_count, grp_count, first,
    normed, cosine, sine, starts, meta, resid, own_kv, table, w_query, w_out, pages,
    middle, arrived, tables,
    wq, wo, kv, total, query, att, mixed, outgoing, incoming,
    qsem, wsem, ring_send, ring_recv, side_send, side_recv, send, recv,
    self_sem, psend, precv, tsend, trecv,
):
    tp = lax.axis_index("tp")
    grp = lax.axis_index("grp")
    core = grp % 2
    tok, width = resid.shape
    reach = grp_count // 2
    window = (reach + 1) * tok
    load_q = [pltpu.make_async_copy(w_query.at[e], wq.at[e], qsem.at[e]) for e in range(E_ATT)]
    load_w = [
        pltpu.make_async_copy(w_out.at[e], wo.at[pl.ds(e * width, width)], wsem.at[e])
        for e in range(E_ATT)
    ]
    for load in load_q + load_w:
        load.start()
    barrier = pltpu.get_barrier_semaphore()
    for j in range(1, tp_count):
        pl.semaphore_signal(
            barrier, inc=1, device_id={"tp": (tp + j) % tp_count}, device_id_type=MESH
        )
    for j in range(1, grp_count):
        pl.semaphore_signal(
            barrier, inc=1, device_id={"grp": (grp + j) % grp_count}, device_id_type=MESH
        )
    kv[reach] = own_kv[...]
    pl.semaphore_wait(barrier, tp_count - 1 + grp_count - 1)

    hops = reach // 2
    onward = {"grp": (grp + 2) % grp_count}
    other = {"grp": grp + 1 - 2 * core}

    def ring(h):
        return pltpu.make_async_remote_copy(
            kv.at[reach - 2 * h], kv.at[reach - 2 * h - 2],
            ring_send.at[h], ring_recv.at[h], onward, MESH,
        )

    def side(n):
        return pltpu.make_async_remote_copy(
            kv.at[reach - 2 * (core + n)], kv.at[reach - 1 - 2 * n],
            side_send.at[n], side_recv.at[n], other, MESH,
        )

    rings = [ring(h) for h in range(hops)]
    sides = [side(n) for n in range(hops)]
    rings[0].start()

    table_copies = []
    for j in range(1, grp_count):
        table_copies.append(
            pltpu.make_async_remote_copy(
                table, tables.at[grp], tsend.at[j - 1], trecv.at[j - 1],
                {"grp": (grp + j) % grp_count}, MESH,
            )
        )
    for copy in table_copies:
        copy.start()
    tables[grp] = table[...]

    ids = meta[...].astype(jnp.float32)
    total[...] = jnp.zeros_like(total)
    for e in range(E_ATT):
        load_q[e].wait()
        projected = jnp.dot(normed[...], wq[e], preferred_element_type=jnp.float32)
        for k in range(TOPK):
            total[k] = jnp.where(
                ids[:, first + k : first + k + 1] == float(e), projected, total[k]
            )
    for k in range(TOPK):
        query[k] = turn_heads(total[k], cosine[...], sine[...], width // HD).astype(jnp.bfloat16)
    column = lax.broadcasted_iota(jnp.int32, (tok, window), 1) + (grp - reach) * tok
    row = lax.broadcasted_iota(jnp.int32, (tok, window), 0) + grp * tok
    live = (column <= row) & (column >= starts[...])
    bias = jnp.where(live, 0.0, masked_score)
    for h in range(hops):
        rings[h].wait_recv()
        if h + 1 < hops:
            rings[h + 1].start()
        sides[h].start()
    for h in range(hops):
        sides[h].wait_recv()
    page_copies = send_pages(grp_count, slice(0, 1), pages, arrived, self_sem, psend, precv)
    scale = HD ** (-0.5)
    for head in range(width // HD):
        lanes = slice(head * HD, (head + 1) * HD)
        key_head = kv[:, :, lanes].reshape(window, HD)
        value_head = kv[:, :, width + head * HD : width + (head + 1) * HD].reshape(window, HD)
        for k in range(TOPK):
            scores = lax.dot_general(
                query[k, :, lanes], key_head, (((1,), (1,)), ((), ())),
                preferred_element_type=jnp.float32,
            ) + bias
            top = jnp.max(scores, axis=-1, keepdims=True)
            weights = jnp.exp((scores - top) * scale)
            weight_sum = jnp.sum(weights, axis=-1, keepdims=True)
            summed = jnp.dot(
                weights.astype(jnp.bfloat16), value_head, preferred_element_type=jnp.float32
            )
            att[k, :, lanes] = summed / weight_sum
    for e in range(E_ATT):
        mix = None
        for k in range(TOPK):
            at = first + k
            gate = jnp.where(
                ids[:, at : at + 1] == float(e), ids[:, at + TOPK : at + TOPK + 1], 0.0
            )
            term = gate * att[k]
            mix = term if mix is None else mix + term
        mixed[:, e * width : (e + 1) * width] = mix.astype(jnp.bfloat16)
    for load in load_w:
        load.wait()
    copies = []
    for j in list(range(1, tp_count)) + [0]:
        peer = (tp + j) % tp_count
        part = jnp.dot(
            mixed[...], wo[:, pl.ds(pl.multiple_of(peer * width, 128), width)],
            preferred_element_type=jnp.float32,
        )
        if j:
            outgoing[j - 1] = part.astype(jnp.bfloat16)
            copy = pltpu.make_async_remote_copy(
                outgoing.at[j - 1], incoming.at[j - 1], send.at[j - 1], recv.at[j - 1],
                {"tp": peer}, MESH,
            )
            copy.start()
            copies.append(copy)
    result = resid[...].astype(jnp.float32) + part
    for j, copy in enumerate(copies):
        copy.wait()
        result = result + incoming[j].astype(jnp.float32)
    middle[...] = result.astype(jnp.bfloat16)
    for copy in rings + sides:
        copy.wait_send()
    for copy in table_copies + page_copies:
        copy.wait()


def expert_kernel(
    tp_count, grp_count, cap, step_blocks,
    select, mid, mix, gain, w_gate, w_up, w_down, pages,
    out, arrived,
    wg, wu, wd, picked, gathered, xn, rs_own, rs_out, rs_in, ret_out, ret_in,
    wsem, self_sem, psend, precv, dsend, drecv, asend, arecv, rsend, rrecv, tsend, trecv,
):
    tp = lax.axis_index("tp")
    grp = lax.axis_index("grp")
    width = mid.shape[1]
    loads = [
        pltpu.make_async_copy(src, dst, wsem.at[i])
        for i, (src, dst) in enumerate(((w_gate, wg), (w_up, wu), (w_down, wd)))
    ]
    for load in loads:
        load.start()
    barrier = pltpu.get_barrier_semaphore()
    for j in range(1, tp_count):
        pl.semaphore_signal(
            barrier, inc=1, device_id={"tp": (tp + j) % tp_count}, device_id_type=MESH
        )
    for j in range(1, grp_count):
        pl.semaphore_signal(
            barrier, inc=1, device_id={"grp": (grp + j) % grp_count}, device_id_type=MESH
        )
    per_owner = grp_count // E_MLP
    step_rows = step_blocks * cap
    steps = grp_count // step_blocks

    picked_rows = None
    for e in range(E_MLP):
        picked_rows = jnp.dot(
            select[e * cap : (e + 1) * cap, :], mid[...], preferred_element_type=jnp.float32
        )
        picked[e] = picked_rows.astype(jnp.bfloat16)
    gathered[tp, 0:cap, :] = picked[grp // per_owner]
    pl.semaphore_wait(barrier, tp_count - 1 + grp_count - 1)
    dispatch = []
    for i in range(1, grp_count):
        peer = (grp + grp_count - i) % grp_count
        copy = pltpu.make_async_remote_copy(
            picked.at[peer // per_owner], gathered.at[tp, pl.ds(i * cap, cap)],
            dsend.at[i - 1], drecv.at[i - 1], {"grp": peer}, MESH,
        )
        copy.start()
        dispatch.append(copy)

    ag = []

    def spread(step):
        rows = pl.ds(step * step_rows, step_rows)
        ag.append([])
        for j in range(1, tp_count):
            copy = pltpu.make_async_remote_copy(
                gathered.at[tp, rows], gathered.at[tp, rows],
                asend.at[step, j - 1], arecv.at[step, j - 1],
                {"tp": (tp + j) % tp_count}, MESH,
            )
            copy.start()
            ag[step].append(copy)

    def pass_on(step):
        for i in range(step * step_blocks, (step + 1) * step_blocks):
            if i:
                dispatch[i - 1].wait_recv()
        spread(step)

    pass_on(0)
    rs = []
    ret = []

    def give_back(step):
        rows = slice(step * step_rows, (step + 1) * step_rows)
        total = rs_own[rows, :]
        for j in range(tp_count - 1):
            rs[step][j].wait_recv()
            total = total + rs_in[j, rows, :].astype(jnp.float32)
        ret_out[rows, :] = total.astype(jnp.bfloat16)
        for i in range(step * step_blocks, (step + 1) * step_blocks):
            part = slice(i * cap, (i + 1) * cap)
            mine = pl.ds(pl.multiple_of(grp * cap, cap), cap)
            if i == 0:
                ret_in[mine, :] = ret_out[part, :]
            else:
                copy = pltpu.make_async_remote_copy(
                    ret_out.at[pl.ds(i * cap, cap)], ret_in.at[mine],
                    tsend.at[i - 1], trecv.at[i - 1],
                    {"grp": (grp + i) % grp_count}, MESH,
                )
                copy.start()
                ret.append(copy)

    page_copies = []
    for step in range(steps):
        rows = slice(step * step_rows, (step + 1) * step_rows)
        if step + 1 < steps:
            pass_on(step + 1)
        if step == 0 and pages.shape[1] > 1:
            page_copies = send_pages(
                grp_count, slice(1, None), pages, arrived, self_sem, psend, precv
            )
        for copy in ag[step]:
            copy.wait_recv()
        if step == 0:
            for load in loads:
                load.wait()
        square = None
        for s in range(tp_count):
            part = gathered[s, rows, :].astype(jnp.float32)
            term = jnp.sum(part * part, axis=-1, keepdims=True)
            square = term if square is None else square + term
        factor = lax.rsqrt(square * (1.0 / (tp_count * width)) + epsilon)
        for s in range(tp_count):
            lanes = slice(s * width, (s + 1) * width)
            xn[:, lanes] = (
                gathered[s, rows, :].astype(jnp.float32) * factor * gain[:, lanes]
            ).astype(jnp.bfloat16)
        gate = jnp.dot(xn[...], wg[...], preferred_element_type=jnp.float32)
        up = jnp.dot(xn[...], wu[...], preferred_element_type=jnp.float32)
        hidden = (gate / (1.0 + jnp.exp(-gate)) * up).astype(jnp.bfloat16)
        rs.append([])
        for j in list(range(1, tp_count)) + [0]:
            peer = (tp + j) % tp_count
            part = jnp.dot(
                hidden, wd[:, pl.ds(pl.multiple_of(peer * width, 128), width)],
                preferred_element_type=jnp.float32,
            )
            if j:
                rs_out[j - 1, rows, :] = part.astype(jnp.bfloat16)
                span = pl.ds(step * step_rows, step_rows)
                copy = pltpu.make_async_remote_copy(
                    rs_out.at[j - 1, span], rs_in.at[j - 1, span],
                    rsend.at[step, j - 1], rrecv.at[step, j - 1],
                    {"tp": peer}, MESH,
                )
                copy.start()
                rs[step].append(copy)
            else:
                rs_own[rows, :] = part
        if step:
            give_back(step - 1)
    give_back(steps - 1)
    for copy in ret:
        copy.wait()
    for copy in dispatch:
        copy.wait_send()
    for group in ag + rs:
        for copy in group:
            copy.wait_send()
    out[...] = (
        mid[...].astype(jnp.float32)
        + lax.dot_general(
            mix[...], ret_in[...], (((0,), (0,)), ((), ())), preferred_element_type=jnp.float32
        )
    ).astype(jnp.bfloat16)
    for copy in page_copies:
        copy.wait()


def pick_pages_kernel(order, pages, picked, held, isem, osem):
    count = pages.shape[0]
    reads = [
        pltpu.make_async_copy(pages.at[order[i]], held.at[i], isem.at[i]) for i in range(count)
    ]
    writes = [pltpu.make_async_copy(held.at[i], picked.at[i], osem.at[i]) for i in range(count)]
    for copy in reads:
        copy.start()
    for read, write in zip(reads, writes):
        read.wait()
        write.start()
    for copy in writes:
        copy.wait()


def place_pages_kernel(slot_of, *refs):
    parts, (placed, held, isem, osem) = refs[:-4], refs[-4:]
    reads = []
    for part in parts:
        for i in range(part.shape[0]):
            at = len(reads)
            reads.append(pltpu.make_async_copy(part.at[i], held.at[at], isem.at[at]))
    writes = [
        pltpu.make_async_copy(held.at[i], placed.at[slot_of[i]], osem.at[i])
        for i in range(len(reads))
    ]
    for copy in reads:
        copy.start()
    for read, write in zip(reads, writes):
        read.wait()
        write.start()
    for copy in writes:
        copy.wait()


def on_device(
    stream,
    lengths,
    att_routes,
    att_gate,
    mlp_routes,
    mlp_gate,
    gain_attn,
    gain_mlp,
    w_query,
    w_key,
    w_value,
    w_output,
    w_gate,
    w_up,
    w_down,
    cache_in,
    page_table,
):
    grp_count = lax.axis_size("grp")
    tp_count = lax.axis_size("tp")
    grp_index = lax.axis_index("grp")
    rows, model_width = stream.shape
    tok = rows * tp_count
    total_tok = tok * grp_count
    width = w_key.shape[1]
    pages_dev = page_table.shape[0]
    bf16 = jnp.bfloat16
    f32 = jnp.float32
    dma = pltpu.SemaphoreType.DMA
    sds = jax.ShapeDtypeStruct

    query_index = grp_index * tok + jnp.arange(tok, dtype=jnp.int32)
    ends = jnp.sum(
        jnp.where(
            jnp.arange(lengths.shape[0])[None, :] <= jnp.arange(lengths.shape[0])[:, None],
            lengths[None, :], 0,
        ),
        axis=1,
    )
    passed = ends[None, :] <= query_index[:, None]
    starts = jnp.max(jnp.where(passed, ends[None, :], 0), axis=1, keepdims=True)
    position = (query_index[:, None] - starts).astype(f32)
    frequency = rope_base ** (-(jnp.arange(HD // 2, dtype=f32) * 2.0 / HD))
    angles = position * frequency[None, :]
    cos_half, sin_half = jnp.cos(angles), jnp.sin(angles)
    cosine = jnp.concatenate([cos_half, cos_half], axis=1)
    sine = jnp.concatenate([-sin_half, sin_half], axis=1)

    normed, kvm, info, resid = pl.pallas_call(
        functools.partial(key_value_kernel, tp_count),
        out_shape=(
            sds((tok, model_width), bf16),
            sds((tok, 2 * width), bf16),
            sds((tok, META), bf16),
            sds((tok, width), bf16),
        ),
        in_specs=[VM] * 8 + [ANY] * 2,
        out_specs=(VM,) * 4,
        scratch_shapes=[
            pltpu.VMEM((tok, model_width), bf16),
            pltpu.VMEM((rows, META), bf16),
            pltpu.VMEM(w_key.shape, bf16),
            pltpu.VMEM(w_value.shape, bf16),
            dma((2,)),
            dma((tp_count - 1,)),
            dma((tp_count - 1,)),
            dma((tp_count - 1,)),
            dma((tp_count - 1,)),
        ],
        compiler_params=params(1),
        name="gather_key_value",
    )(stream, att_routes, att_gate, mlp_routes, mlp_gate, gain_attn[None, :], cosine, sine, w_key, w_value)

    page_len = tok // pages_dev
    pair_pages = pages_dev // grp_count
    page_blocks = cache_in.reshape((pages_dev, page_len) + cache_in.shape[1:])
    page_ids = jnp.arange(pages_dev, dtype=jnp.int32)
    sort_key = (page_table // pages_dev) * pages_dev + page_ids
    place = jnp.sum((sort_key[None, :] < sort_key[:, None]).astype(jnp.int32), axis=1)
    page_order = jnp.sum(
        jnp.where(place[None, :] == page_ids[:, None], page_ids[None, :], 0), axis=1
    )
    page_sends = pl.pallas_call(
        pick_pages_kernel,
        out_shape=sds(page_blocks.shape, bf16),
        in_specs=[pl.BlockSpec(memory_space=pltpu.SMEM), ANY],
        out_specs=ANY,
        scratch_shapes=[
            pltpu.VMEM(page_blocks.shape, bf16),
            dma((pages_dev,)),
            dma((pages_dev,)),
        ],
        compiler_params=params(),
        name="pick_pages",
    )(page_order, page_blocks).reshape(
        (grp_count, pair_pages) + page_blocks.shape[1:]
    )

    window = (grp_count // 2 + 1) * tok
    early_shape = (grp_count, 1) + page_blocks.shape[1:]
    reach = grp_count // 2
    peers = tp_count - 1
    table = jnp.broadcast_to(jnp.pad(page_table, (0, META - pages_dev))[None, :], (8, META))
    middle, early_pages, tables = pl.pallas_call(
        functools.partial(attend_kernel, tp_count, grp_count, 0),
        out_shape=(
            sds((tok, width), bf16),
            sds(early_shape, bf16),
            sds((grp_count, 8, META), jnp.int32),
        ),
        in_specs=[VM] * 8 + [ANY] * 3,
        out_specs=(VM, ANY, VM),
        scratch_shapes=[
            pltpu.VMEM(w_query.shape, bf16),
            pltpu.VMEM((E_ATT * width, model_width), bf16),
            pltpu.VMEM((reach + 1, tok, 2 * width), bf16),
            pltpu.VMEM((TOPK, tok, width), f32),
            pltpu.VMEM((TOPK, tok, width), bf16),
            pltpu.VMEM((TOPK, tok, width), f32),
            pltpu.VMEM((tok, E_ATT * width), bf16),
            pltpu.VMEM((peers, tok, width), bf16),
            pltpu.VMEM((peers, tok, width), bf16),
            dma((E_ATT,)),
            dma((E_ATT,)),
            dma((reach // 2,)),
            dma((reach // 2,)),
            dma((reach // 2,)),
            dma((reach // 2,)),
            dma((peers,)),
            dma((peers,)),
            dma((1,)),
            dma((grp_count - 1,)),
            dma((grp_count - 1,)),
            dma((grp_count - 1,)),
            dma((grp_count - 1,)),
        ],
        compiler_params=params(2),
        name="attend",
    )(normed, cosine, sine, starts, info, resid, kvm, table, w_query, w_output, page_sends)

    capacity = tok * TOPK * 5 // (E_MLP * 4)
    per_owner = grp_count // E_MLP
    lower = (jnp.arange(tok)[:, None] < jnp.arange(tok)[None, :]).astype(bf16)
    slot_ids = jnp.arange(capacity, dtype=jnp.int32)
    at = 2 * TOPK
    own_ids = info[:, at : at + TOPK].astype(jnp.int32).T
    own_gate = info[:, at + TOPK : at + 2 * TOPK].astype(f32).T
    expert_ids = jnp.arange(E_MLP, dtype=jnp.int32)
    own_hot = own_ids[None, :, :] == expert_ids[:, None, None]
    own_weight = jnp.sum(jnp.where(own_hot, own_gate[None, :, :], 0.0), axis=1)
    own_hit = jnp.any(own_hot, axis=1)
    own_rank = jnp.dot(own_hit.astype(bf16), lower, preferred_element_type=f32).astype(jnp.int32)
    placed = own_hit[:, None, :] & (own_rank[:, None, :] == slot_ids[None, :, None])
    select = placed.astype(bf16).reshape(E_MLP * capacity, tok)
    mix = jnp.where(placed, own_weight[:, None, :], 0.0).astype(bf16)
    mix = jnp.repeat(mix, per_owner, axis=0).reshape(grp_count * capacity, tok)

    hid = w_gate.shape[1]
    late_shape = (grp_count, max(pair_pages - 1, 1)) + page_blocks.shape[1:]
    step_blocks = 2
    steps = grp_count // step_blocks
    slots = grp_count * capacity
    peers = tp_count - 1
    hidden_out, late_pages = pl.pallas_call(
        functools.partial(expert_kernel, tp_count, grp_count, capacity, step_blocks),
        out_shape=(sds((tok, width), bf16), sds(late_shape, bf16)),
        in_specs=[VM] * 4 + [ANY] * 4,
        out_specs=(VM, ANY),
        scratch_shapes=[
            pltpu.VMEM((model_width, hid), bf16),
            pltpu.VMEM((model_width, hid), bf16),
            pltpu.VMEM((hid, model_width), bf16),
            pltpu.VMEM((E_MLP, capacity, width), bf16),
            pltpu.VMEM((tp_count, slots, width), bf16),
            pltpu.VMEM((step_blocks * capacity, model_width), bf16),
            pltpu.VMEM((slots, width), f32),
            pltpu.VMEM((peers, slots, width), bf16),
            pltpu.VMEM((peers, slots, width), bf16),
            pltpu.VMEM((slots, width), bf16),
            pltpu.VMEM((slots, width), bf16),
            dma((3,)),
            dma((1,)),
            dma((grp_count - 1,)),
            dma((grp_count - 1,)),
            dma((grp_count - 1,)),
            dma((grp_count - 1,)),
            dma((steps, peers)),
            dma((steps, peers)),
            dma((steps, peers)),
            dma((steps, peers)),
            dma((grp_count - 1,)),
            dma((grp_count - 1,)),
        ],
        compiler_params=params(3),
        name="experts",
    )(select, middle, mix, gain_mlp[None, :], w_gate, w_up, w_down, page_sends)

    tables = tables[:, 0, :pages_dev].reshape(-1)
    here = tables // pages_dev == grp_index
    all_ids = jnp.arange(tables.shape[0], dtype=jnp.int32)
    arrival = jnp.sum(
        (here[None, :] & (all_ids[None, :] < all_ids[:, None])).astype(jnp.int32), axis=1
    )
    source = arrival // pair_pages
    within = arrival % pair_pages
    arrival = jnp.where(
        within == 0, source, grp_count + source * (pair_pages - 1) + within - 1
    )
    local = tables % pages_dev
    slot_of = jnp.sum(
        jnp.where(here[None, :] & (arrival[None, :] == page_ids[:, None]), local[None, :], 0),
        axis=1,
    )
    parts = [early_pages] if pair_pages == 1 else [early_pages, late_pages]
    parts = [part.reshape((-1,) + page_blocks.shape[1:]) for part in parts]
    cache_out = pl.pallas_call(
        place_pages_kernel,
        out_shape=sds(page_blocks.shape, bf16),
        in_specs=[pl.BlockSpec(memory_space=pltpu.SMEM)] + [ANY] * len(parts),
        out_specs=ANY,
        scratch_shapes=[
            pltpu.VMEM(page_blocks.shape, bf16),
            dma((pages_dev,)),
            dma((pages_dev,)),
        ],
        compiler_params=params(),
        name="place_pages",
    )(slot_of, *parts)
    return (hidden_out, cache_out)


def solution(mesh):
    return jax.shard_map(
        on_device,
        mesh=mesh,
        in_specs=(
            P(("grp", "tp"), None),
            P(),
            P(("grp", "tp"), None),
            P(("grp", "tp"), None),
            P(("grp", "tp"), None),
            P(("grp", "tp"), None),
            P(),
            P(),
            P(None, None, "tp"),
            P(None, "tp"),
            P(None, "tp"),
            P(None, "tp", None),
            P(None, ("grp", "tp")),
            P(None, ("grp", "tp")),
            P(("grp", "tp"), None),
            P("grp", None, None, "tp", None),
            P("grp"),
        ),
        out_specs=(P("grp", "tp"), P("grp", None, None, None, "tp", None)),
        check_vma=False,
    )
```
